32 devices in a mesh: row: 4 (over y, x), col: 8 (over z, core).
Axes of the slice: x: 2, y: 2, z: 4, core: 2. Of those that a mesh axis runs over, the one named last changes fastest.
Arguments:
- tokens: bfloat16 [1024, 6144], P('col', 'row'), may hold values from -6 to 6
- learning_rate: float32 [1], replicated, may hold values from 0.05 to 0.5
- weight_in: bfloat16 [6144, 24576], P('row', 'col'), may hold values from -0.078125 to 0.078125
- grad_in: bfloat16 [6144, 24576], P('row', 'col'), may hold values from -6 to 6
- moment_in: bfloat16 [6144, 24576], P('row', 'col'), may hold values from -4 to 4
- second_in: bfloat16 [6144, 24576], P('row', 'col'), may hold values from 0.25 to 4
- weight_out: bfloat16 [24576, 6144], P('col', 'row'), may hold values from -0.0390625 to 0.0390625
- grad_out: bfloat16 [24576, 6144], P('col', 'row'), may hold values from -6 to 6
- moment_out: bfloat16 [24576, 6144], P('col', 'row'), may hold values from -4 to 4
- second_out: bfloat16 [24576, 6144], P('col', 'row'), may hold values from 0.25 to 4
Outputs:
- block_out: bfloat16 [1024, 6144], P('col', 'row')
- block_tangent: bfloat16 [1024, 6144], P('col', 'row')
The draws below stay inside these ranges and needn't reach their ends.
All inputs are finite; a program needn't handle non-finite values.
Results may differ from the reference program's by a relative error of at most 0.025.
Values may be sent and summed in bfloat16 or wider, within the bound.
A program may use at most 192 MiB of HBM per device.

```python
import math
import jax
import jax.numpy as jnp
from jax import lax

D = 6144
FF = 24576
TOKENS = 1024
N_ROW = 4
N_COL = 8


def shard_levels(stream_key, shape, cuts, low, largest):
    def one(dim, blocks):
        draws = jax.random.uniform(jax.random.fold_in(jax.random.fold_in(stream_key, 6), dim), (blocks,), jnp.float32, low / len(cuts), largest / len(cuts))
        return jnp.repeat(jnp.exp(draws), shape[dim] // blocks).reshape((-1,) + (1,) * (len(shape) - dim - 1))

    gain = one(*cuts[0])
    for cut in cuts[1:]:
        gain = gain * one(*cut)
    return gain


def scatter_about(own_key, dims, scale, most, cuts=(), kind=jnp.bfloat16):
    result = jax.random.normal(own_key, dims, jnp.float32) * scale
    if len(cuts) > 0:
        result = shard_levels(own_key, dims, cuts, -0.22, 0.18) * result
    return jnp.clip(result, min=-most, max=most).astype(kind)


def setup_inputs(seed: int = 0) -> dict:
    splits = jax.random.split(jax.random.key(seed), 11)
    tokens = scatter_about(splits[0], (TOKENS, D), 1.0, 6.0, ((0, 8), (1, 4)))
    learning_rate = jnp.clip(jnp.exp(jax.random.uniform(splits[1], (1,), jnp.float32, math.log(0.05), math.log(0.5))), 0.05, 0.5)
    weight_in = scatter_about(splits[2], (D, FF), D ** -0.5, 0.078125, ((0, 4), (1, 8)))
    grad_in = scatter_about(splits[3], (D, FF), 1.0, 6.0, ((0, 4), (1, 8)))
    moment_in = scatter_about(splits[4], (D, FF), 0.5, 4.0, ((0, 4), (1, 8)))
    second_in = jnp.clip(jnp.exp(math.log(4.0) - 2.7725887 * jax.random.uniform(splits[5], (D, FF), jnp.float32) ** shard_levels(splits[5], (D, FF), ((0, 4), (1, 8)), -0.2, 0.2)), 0.25, 4.0).astype(jnp.bfloat16)
    weight_out = scatter_about(splits[6], (FF, D), FF ** -0.5, 0.0390625, ((0, 8), (1, 4)))
    grad_out = scatter_about(splits[7], (FF, D), 1.0, 6.0, ((0, 8), (1, 4)))
    moment_out = scatter_about(splits[8], (FF, D), 0.5, 4.0, ((0, 8), (1, 4)))
    second_out = jnp.clip(jnp.exp(math.log(4.0) - 2.7725887 * jax.random.uniform(splits[9], (FF, D), jnp.float32) ** shard_levels(splits[9], (FF, D), ((0, 8), (1, 4)), -0.2, 0.2)), 0.25, 4.0).astype(jnp.bfloat16)
    return dict(tokens=tokens, learning_rate=learning_rate, weight_in=weight_in, grad_in=grad_in, moment_in=moment_in, second_in=second_in, weight_out=weight_out, grad_out=grad_out, moment_out=moment_out, second_out=second_out)


first_decay = 0.9
second_decay = 0.95
first_fix = 1.0 - 0.9 ** 20
second_fix = 1.0 - 0.95 ** 20
epsilon = 1e-08
gelu_coeff = math.sqrt(2.0 / math.pi)

def adam_direction(grad, moment, second, scale):
    grad_wide = grad.astype(jnp.float32)
    moment_new = first_decay * moment.astype(jnp.float32) + (1.0 - first_decay) * grad_wide
    second_new = second_decay * second.astype(jnp.float32) + (1.0 - second_decay) * grad_wide * grad_wide
    return -scale * (moment_new / first_fix) / (jnp.sqrt(second_new / second_fix) + epsilon)

def activate(hidden_pair, width):
    hidden = hidden_pair[:, :width]
    hidden_tan = hidden_pair[:, width:]
    inner = gelu_coeff * (hidden + 0.044715 * hidden * hidden * hidden)
    shaped = jnp.tanh(inner)
    value = 0.5 * hidden * (1.0 + shaped)
    slope = 0.5 * (1.0 + shaped) + 0.5 * hidden * (1.0 - shaped * shaped) * gelu_coeff * (1.0 + 3.0 * 0.044715 * hidden * hidden)
    return (value.astype(jnp.bfloat16), (slope * hidden_tan).astype(jnp.bfloat16))

def reference(tokens, learning_rate, weight_in, grad_in, moment_in, second_in, weight_out, grad_out, moment_out, second_out):
    rate = learning_rate[0]
    dir_in = adam_direction(grad_in, moment_in, second_in, 1.0 / math.sqrt(D))
    new_in = (weight_in.astype(jnp.float32) + rate * dir_in).astype(jnp.bfloat16)
    delta_in = dir_in.astype(jnp.bfloat16)
    dir_out = adam_direction(grad_out, moment_out, second_out, 1.0 / math.sqrt(FF))
    new_out = (weight_out.astype(jnp.float32) + rate * dir_out).astype(jnp.bfloat16)
    delta_out = dir_out.astype(jnp.bfloat16)
    block_d = D // N_ROW
    block_f = FF // N_COL

    def first_block(index, total):
        begin = index * block_d
        rows_x = lax.dynamic_slice_in_dim(tokens, begin, block_d, 1)
        rows_w = lax.dynamic_slice_in_dim(new_in, begin, block_d, 0)
        rows_d = lax.dynamic_slice_in_dim(delta_in, begin, block_d, 0)
        part = jnp.concatenate([jnp.dot(rows_x, rows_w, preferred_element_type=jnp.float32), jnp.dot(rows_x, rows_d, preferred_element_type=jnp.float32)], axis=1)
        part = lax.optimization_barrier(part.astype(jnp.bfloat16))
        return total + part.astype(jnp.float32)
    hidden_pair = lax.fori_loop(0, N_ROW, first_block, jnp.zeros((TOKENS, 2 * FF), jnp.float32))
    value, tangent = activate(hidden_pair, FF)

    def second_block(index, total):
        begin = index * block_f
        cols_v = lax.dynamic_slice_in_dim(value, begin, block_f, 1)
        cols_t = lax.dynamic_slice_in_dim(tangent, begin, block_f, 1)
        rows_w = lax.dynamic_slice_in_dim(new_out, begin, block_f, 0)
        rows_d = lax.dynamic_slice_in_dim(delta_out, begin, block_f, 0)
        primal = jnp.dot(cols_v, rows_w, preferred_element_type=jnp.float32)
        along = jnp.dot(cols_t, rows_w, preferred_element_type=jnp.float32) + jnp.dot(cols_v, rows_d, preferred_element_type=jnp.float32)
        part = jnp.concatenate([primal, along], axis=1)
        part = lax.optimization_barrier(part.astype(jnp.bfloat16))
        return total + part.astype(jnp.float32)
    out_pair = lax.fori_loop(0, N_COL, second_block, jnp.zeros((TOKENS, 2 * D), jnp.float32))
    return (out_pair[:, :D].astype(jnp.bfloat16), out_pair[:, D:].astype(jnp.bfloat16))
```

```python
import math

import jax
import jax.numpy as jnp
from jax import lax
from jax.sharding import PartitionSpec as P


first_decay = 0.9
second_decay = 0.95
first_fix = 1.0 - 0.9**20
second_fix = 1.0 - 0.95**20
epsilon = 1e-08
gelu_coeff = math.sqrt(2.0 / math.pi)

MOST_CHUNKS = 4
PIECES = 2


def adam_direction(grad, moment, second, scale):
    grad_wide = grad.astype(jnp.float32)
    moment_new = first_decay * moment.astype(jnp.float32) + (1.0 - first_decay) * grad_wide
    second_new = (
        second_decay * second.astype(jnp.float32) + (1.0 - second_decay) * grad_wide * grad_wide
    )
    return -scale * (moment_new / first_fix) / (jnp.sqrt(second_new / second_fix) + epsilon)


def adam(weight, grad, moment, second, rate, fan_in):
    direction = adam_direction(grad, moment, second, 1.0 / math.sqrt(fan_in))
    new = (weight.astype(jnp.float32) + rate * direction).astype(jnp.bfloat16)
    return lax.optimization_barrier((new, direction.astype(jnp.bfloat16)))


def activate(hidden, hidden_tan):
    inner = gelu_coeff * (hidden + 0.044715 * hidden * hidden * hidden)
    shaped = jnp.tanh(inner)
    value = 0.5 * hidden * (1.0 + shaped)
    slope = 0.5 * (1.0 + shaped) + 0.5 * hidden * (1.0 - shaped * shaped) * gelu_coeff * (
        1.0 + 3.0 * 0.044715 * hidden * hidden
    )
    return (value.astype(jnp.bfloat16), (slope * hidden_tan).astype(jnp.bfloat16))


def add(a, b):
    return a.astype(jnp.float32) + b.astype(jnp.float32)


def swap(block, axis, n, bit):
    return lax.ppermute(block, axis, [(i, i ^ (1 << bit)) for i in range(n)])


def shifted(block, n_col, shift):
    return lax.ppermute(block, "col", [(i, (i + 2 * shift) % n_col) for i in range(n_col)])


def scatter_row(part, n_row, order):
    me = lax.axis_index("row")
    bits = sorted(order, reverse=True)
    blocks = part.reshape((2,) * len(bits) + part.shape[1:])
    for step, bit in enumerate(order):
        place = bits.index(bit)
        bits.remove(bit)
        mine = lax.rem(lax.div(me, 1 << bit), 2)
        keep = lax.dynamic_index_in_dim(blocks, mine, place, False)
        give = lax.dynamic_index_in_dim(blocks, 1 - mine, place, False)
        blocks = add(keep, swap(give, "row", n_row, bit))
        if step < len(order) - 1:
            blocks = blocks.astype(jnp.bfloat16)
    return blocks


def gather_row(block, n_row, order):
    held = block[None]
    done = []
    for bit in order:
        arrived = swap(held, "row", n_row, bit)
        held = jnp.concatenate([held, arrived], axis=0)
        done.append(bit)
    shape = (2,) * len(done) + block.shape
    held = held.reshape(shape)
    axes = done[::-1]
    perm = [axes.index(b) for b in sorted(done, reverse=True)]
    held = held.transpose(perm + list(range(len(done), len(shape))))
    return held.reshape((n_row,) + block.shape)


def gather_col(block, n_col):
    n_chip = n_col // 2
    me = lax.axis_index("col")
    core, chip = lax.rem(me, 2), lax.div(me, 2)
    held = [block]
    for shift in range(1, n_chip):
        held.append(shifted(block, n_col, shift))
    stacked = jnp.stack(held[::-1] * 2)
    line = lax.dynamic_slice_in_dim(stacked, n_chip - 1 - chip, n_chip, 0)
    other = swap(line, "col", n_col, 0)
    first = jnp.where(core == 0, line, other)
    second = jnp.where(core == 0, other, line)
    return jnp.stack([first, second], axis=1).reshape((n_col,) + block.shape)


def core_sum(part, n_col):
    core = lax.rem(lax.axis_index("col"), 2)
    blocks = part.reshape((n_col // 2, 2) + part.shape[1:])
    mine = lax.dynamic_index_in_dim(blocks, core, 1, False)
    other = lax.dynamic_index_in_dim(blocks, 1 - core, 1, False)
    return add(mine, swap(other, "col", n_col, 0)).astype(jnp.bfloat16)


def line_send(pair, n_col):
    n_chip = n_col // 2
    chip = lax.div(lax.axis_index("col"), 2)
    terms = [lax.dynamic_index_in_dim(pair, chip, 0, False)]
    for shift in range(1, n_chip):
        block = lax.dynamic_index_in_dim(pair, lax.rem(chip + shift, n_chip), 0, False)
        terms.append(shifted(block, n_col, shift))
    return terms


def chunk_count(local_tokens, n_row):
    return max(1, min(MOST_CHUNKS, local_tokens // n_row))


def make_body(n_row, n_col):
    up = list(range(n_row.bit_length() - 1))
    down = up[::-1]

    def body(
        tokens,
        learning_rate,
        weight_in,
        grad_in,
        moment_in,
        second_in,
        weight_out,
        grad_out,
        moment_out,
        second_out,
    ):
        rate = learning_rate[0]
        depth, local_ff = weight_in.shape
        local_d = weight_out.shape[1]
        chunks = chunk_count(tokens.shape[0], n_row)
        small = tokens.shape[0] // (chunks * n_row)
        per_piece = chunks // PIECES
        held = []
        for k in range(PIECES):
            rows = tokens.shape[0] // PIECES
            piece = gather_col(tokens[k * rows : (k + 1) * rows], n_col)
            piece = piece.reshape(n_col, per_piece, n_row, small, depth)
            piece = piece.transpose(1, 2, 0, 3, 4).reshape(per_piece, -1, depth)
            held.extend(piece[i] for i in range(per_piece))
        new_in, delta_in = adam(
            weight_in, grad_in, moment_in, second_in, rate, depth * n_row
        )
        shares = []
        for c in range(chunks):
            pair = []
            for w, order in ((new_in, up), (delta_in, down)):
                part = jnp.dot(held[c], w, preferred_element_type=jnp.float32)
                part = part.astype(jnp.bfloat16).reshape(n_row, -1, local_ff)
                pair.append(scatter_row(part, n_row, order))
            shares.append(pair)
        new_out, delta_out = adam(
            weight_out, grad_out, moment_out, second_out, rate, weight_out.shape[0] * n_col
        )
        lines = []
        for c in range(chunks):
            value, tangent = activate(*shares[c])
            value = gather_row(value, n_row, down).reshape(-1, local_ff)
            tangent = gather_row(tangent, n_row, up).reshape(-1, local_ff)
            primal = jnp.dot(value, new_out, preferred_element_type=jnp.float32)
            along = jnp.dot(tangent, new_out, preferred_element_type=jnp.float32) + jnp.dot(
                value, delta_out, preferred_element_type=jnp.float32
            )
            part = jnp.concatenate(
                [primal.astype(jnp.bfloat16), along.astype(jnp.bfloat16)], axis=1
            )
            part = part.reshape(n_row, n_col, small, 2 * local_d).transpose(1, 0, 2, 3)
            part = part.reshape(n_col, n_row * small, 2 * local_d)
            pair = core_sum(part, n_col)
            lines.append(line_send(pair, n_col))
        me = lax.axis_index("row")
        places = jnp.arange(n_row) ^ me
        results = []
        for terms in lines:
            total = terms[0].astype(jnp.float32)
            for term in terms[1:]:
                total += term.astype(jnp.float32)
            total = total.astype(jnp.bfloat16).reshape(n_row, small, -1)
            results.append(jnp.take(total, places, axis=0, mode="clip").reshape(n_row * small, -1))
        result = jnp.concatenate(results, axis=0)
        return (result[:, :local_d], result[:, local_d:])

    return body


def solution(mesh):
    n_row, n_col = mesh.shape["row"], mesh.shape["col"]
    return jax.shard_map(
        make_body(n_row, n_col),
        mesh=mesh,
        in_specs=(
            P("col", "row"),
            P(),
            P("row", "col"),
            P("row", "col"),
            P("row", "col"),
            P("row", "col"),
            P("col", "row"),
            P("col", "row"),
            P("col", "row"),
            P("col", "row"),
        ),
        out_specs=(P("col", "row"), P("col", "row")),
        check_vma=False,
    )
```
